32 devices in a mesh: dom: 4 (over y, x), freq: 8 (over z, core).
Axes of the slice: x: 2, y: 2, z: 4, core: 2. Of those that a mesh axis runs over, the one named last changes fastest.
Arguments:
- voltages: float32 [512, 8192], P('freq', 'dom'), may hold values from -5 to 5
- sources: float32 [512, 8192], P('freq', 'dom'), may hold values from -20 to 20
- terminals: int32 [2, 16384], P(None, 'dom'), may hold values from 0 to 2559, as said below
- elem_current: float32 [2, 16384], P(None, 'dom'), may hold values from 0.2 to 2
- elem_charge: float32 [2, 16384], P(None, 'dom'), may hold values from 0.1 to 1
- jacobi: float32 [256, 2, 2, 8192], P('freq', None, None, 'dom'), may hold values from -1.2 to 2
Outputs:
- residual: float32 [512, 8192], P('freq', 'dom')
- newton_step: float32 [512, 8192], P('freq', 'dom')
- residual_norm: float32 [], replicated
The draws below stay inside these ranges and needn't reach their ends.
Inputs may be any that keep to these rules, and one draw needn't show every extreme that they name: `terminals`: A terminal value below 2048 is a node of the element's own partition; a value v of 2048 or more is node (v - 2048) % 128 of partition (v - 2048) // 128, one of that partition's first 128 nodes.
All inputs are finite; a program needn't handle non-finite values.
Results may differ from the reference program's by a relative error of at most 0.0003.
Values sent between devices are 32-bit elements; how exact they have to be, the bound alone decides.
A program may use at most 64 MiB of HBM per device.

```python
import math
import jax
import jax.numpy as jnp
from jax import lax

S = 512
NPD = 2048
NE = 4096
NB = 128
H = 256
NODES = 8192
NBT = 512
ELEMS = 16384
N_DOM = 4


def draw_terminals(key, part):
    first_key, other_key, remote_key, pick_key = jax.random.split(key, 4)
    first = jax.random.randint(first_key, (ELEMS,), 0, NPD)
    local_other = jax.random.randint(other_key, (ELEMS,), 0, NPD)
    remote = NPD + jax.random.randint(remote_key, (ELEMS,), 0, NBT)
    picked = jax.random.randint(pick_key, (ELEMS,), 0, 4) == 0
    second = jnp.where(picked, remote, local_other)
    first = first.at[0].set(0)
    second = second.at[0].set(NPD + NBT - 1)
    return jnp.stack([first, second]).astype(jnp.int32)


def draw_sources(key, part):
    base_key = jax.random.fold_in(key, 0)
    rows = jnp.arange(S, dtype=jnp.float32) / (S - 1)
    columns = jnp.arange(NODES, dtype=jnp.float32) / (NODES - 1)
    scale = 0.5 * (1.0 + 2.0 * rows)[:, None] * (1.0 + 2.0 * columns)[None, :]
    base = jax.random.truncated_normal(base_key, -4.0, 4.0, (S, NODES), jnp.float32)
    return (base * scale).astype(jnp.float32)


def draw_jacobi(key, part):
    keys = jax.random.split(key, 6)
    shape = (H, NODES)
    bottom = 0.5
    top = 2.0
    low_off = 0.25
    high_off = 0.6
    diag_one = jnp.exp(jax.random.uniform(keys[0], shape, jnp.float32, math.log(bottom), math.log(top)))
    diag_two = jnp.exp(jax.random.uniform(keys[1], shape, jnp.float32, math.log(bottom), math.log(top)))
    mix_one = jax.random.uniform(keys[2], shape, jnp.float32, low_off, high_off)
    mix_two = jax.random.uniform(keys[3], shape, jnp.float32, low_off, high_off)
    sign_one = jnp.where(jax.random.randint(keys[4], shape, 0, 2) == 0, -1.0, 1.0)
    sign_two = jnp.where(jax.random.randint(keys[5], shape, 0, 2) == 0, -1.0, 1.0)
    mean_diag = jnp.sqrt(diag_one * diag_two)
    off_one = sign_one * mix_one * mean_diag
    off_two = sign_two * mix_two * mean_diag
    upper = jnp.stack([diag_one, off_one], axis=1)
    lower = jnp.stack([off_two, diag_two], axis=1)
    return jnp.stack([upper, lower], axis=1).astype(jnp.float32)


def levels(stream_key, dims, cuts, least, largest):
    def one(axis_at, parts):
        heights = jax.random.uniform(jax.random.fold_in(jax.random.fold_in(stream_key, 6), axis_at), (parts,), jnp.float32, least / len(cuts), largest / len(cuts))
        return jnp.repeat(jnp.exp(heights), dims[axis_at] // parts).reshape((-1,) + (1,) * (len(dims) - axis_at - 1))

    gain = one(*cuts[0])
    for cut in cuts[1:]:
        gain = gain * one(*cut)
    return gain


def noise(key, extent, deviation, bound, cuts=(), held_as=jnp.bfloat16):
    level = levels(key, extent, cuts, -0.22, 0.18) if cuts else 1.0
    drawn = jax.random.normal(key, extent, jnp.float32) * deviation * level
    return jnp.minimum(jnp.maximum(drawn, -bound), bound).astype(held_as)


def setup_inputs(seed: int = 0) -> dict:
    splits = jax.random.split(jax.random.key(seed), 7)
    return {
        "voltages": noise(splits[0], (S, NODES), 1.0, 5.0, ((0, 8), (1, 4)), jnp.float32),
        "sources": draw_sources(jax.random.fold_in(splits[6], 71), 0),
        "terminals": draw_terminals(jax.random.fold_in(splits[6], 71), 0),
        "elem_current": jnp.clip(jnp.exp(math.log(2.0) - 2.3025851 * jax.random.uniform(splits[3], (2, ELEMS), jnp.float32) ** levels(splits[3], (2, ELEMS), ((1, 4),), -0.2, 0.2)), 0.2, 2.0),
        "elem_charge": jnp.clip(jnp.exp(math.log(1.0) - 2.3025851 * jax.random.uniform(splits[4], (2, ELEMS), jnp.float32) ** levels(splits[4], (2, ELEMS), ((1, 4),), -0.2, 0.2)), 0.1, 1.0),
        "jacobi": draw_jacobi(jax.random.fold_in(splits[6], 71), 0),
    }


trust_radius = 2.0

def transform_table(samples):
    row_index = jnp.arange(samples, dtype=jnp.int32)
    harmonic = row_index // 2
    is_sine = row_index % 2 == 1
    column = jnp.arange(samples, dtype=jnp.int32)
    order = jnp.where(harmonic == 0, jnp.where(is_sine, samples // 2, 0), harmonic)
    phase = (order[:, None] * column[None, :] % samples).astype(jnp.float32) * (2.0 * math.pi / samples)
    use_sine = is_sine & (harmonic > 0)
    values = jnp.where(use_sine[:, None], jnp.sin(phase), jnp.cos(phase))
    weight = jnp.where(harmonic == 0, math.sqrt(1.0 / samples), math.sqrt(2.0 / samples)).astype(jnp.float32)
    forward = values * weight[:, None]
    pairs = forward.reshape(samples // 2, 2, samples)
    rate = 2.0 / samples * jnp.arange(samples // 2, dtype=jnp.float32)
    derived = jnp.stack([pairs[:, 1], -pairs[:, 0]], axis=1) * rate[:, None, None]
    return jnp.concatenate([forward, derived.reshape(samples, samples)], axis=1)

def reference(voltages, sources, terminals, elem_current, elem_charge, jacobi):
    node_total = voltages.shape[1]

    def partition(totals, index):
        local_terms = lax.dynamic_slice_in_dim(terminals, index * NE, NE, 1)
        cur_params = lax.dynamic_slice_in_dim(elem_current, index * NE, NE, 1)
        chg_params = lax.dynamic_slice_in_dim(elem_charge, index * NE, NE, 1)
        border_id = local_terms - NPD
        remote = border_id // NB * NPD + border_id % NB
        global_terms = jnp.where(local_terms < NPD, index * NPD + local_terms, remote).astype(jnp.int32)
        across = voltages[:, global_terms[0]] - voltages[:, global_terms[1]]
        current = cur_params[0][None, :] * across + cur_params[1][None, :] * jnp.tanh(2.0 * across)
        charge = chg_params[0][None, :] * across + chg_params[1][None, :] * jnp.tanh(across)
        flows = jnp.stack([current, charge])
        totals = totals.at[:, :, global_terms[0]].add(flows)
        totals = totals.at[:, :, global_terms[1]].add(-flows)
        return (totals, None)
    start = jnp.zeros((2, S, node_total), jnp.float32)
    totals, unused = lax.scan(partition, start, jnp.arange(N_DOM, dtype=jnp.int32))
    table = transform_table(S)
    stacked = totals.reshape(2 * S, node_total)
    residual = jnp.dot(table, stacked, precision=lax.Precision.HIGHEST, preferred_element_type=jnp.float32) - sources
    pairs = residual.reshape(S // 2, 2, node_total)
    raw = -(jacobi[:, :, 0, :] * pairs[:, 0:1, :] + jacobi[:, :, 1, :] * pairs[:, 1:2, :])
    raw = raw.reshape(S, node_total)
    squares = jnp.sum(raw * raw)
    spread = jnp.sqrt(squares / (S * node_total) + 1e-06)
    newton_step = raw * jnp.minimum(1.0, trust_radius / spread)
    residual_norm = jnp.sqrt(jnp.sum(residual * residual))
    return (residual, newton_step, residual_norm)
```

```python
import functools
import math

import jax
import jax.numpy as jnp
import numpy as np
from jax import lax
from jax.experimental import pallas as pl
from jax.experimental.pallas import tpu as pltpu
from jax.sharding import PartitionSpec as P

MESH = pl.DeviceIdType.MESH
LANES = 128
VMEM = pltpu.VMEM
trust_radius = 2.0


def fourier_matrix(samples):
    row = np.arange(samples)
    harmonic = row // 2
    sine = row % 2 == 1
    order = np.where(harmonic == 0, np.where(sine, samples // 2, 0), harmonic)
    phase = (order[:, None] * np.arange(samples)[None, :] % samples) * (2.0 * math.pi / samples)
    values = np.where((sine & (harmonic > 0))[:, None], np.sin(phase), np.cos(phase))
    weight = np.where(harmonic == 0, math.sqrt(1.0 / samples), math.sqrt(2.0 / samples))
    full = (values * weight[:, None]).astype(np.float32)
    high = full.astype(jnp.bfloat16)
    low = (full - high.astype(np.float32)).astype(jnp.bfloat16)
    return high, low


def split(x):
    high = x.astype(jnp.bfloat16)
    low = (x - high.astype(jnp.float32)).astype(jnp.bfloat16)
    return high, low


def dot(a, b, contract=((1,), (0,))):
    return lax.dot_general(a, b, (contract, ((), ())), preferred_element_type=jnp.float32)


def flipped(index, mask):
    bit = 1
    while bit <= mask:
        if mask & bit:
            index = index + bit * (1 - 2 * ((index // bit) % 2))
        bit *= 2
    return index


def border_kernel(doms, v_ref, out_ref, send_sem, recv_sem, local_sem):
    me = lax.axis_index("dom")
    barrier = pltpu.get_barrier_semaphore()
    for j in range(1, doms):
        pl.semaphore_signal(barrier, inc=1, device_id={"dom": flipped(me, j)}, device_id_type=MESH)
    pl.semaphore_wait(barrier, doms - 1)
    copies = []
    for j in range(1, doms):
        copy = pltpu.make_async_remote_copy(
            src_ref=v_ref,
            dst_ref=out_ref.at[me],
            send_sem=send_sem.at[j],
            recv_sem=recv_sem.at[me],
            device_id={"dom": flipped(me, j)},
            device_id_type=MESH,
        )
        copy.start()
        copies.append(copy)
    own = pltpu.make_async_copy(v_ref, out_ref.at[me], local_sem)
    own.start()
    own.wait()
    for j in range(1, doms):
        peer = flipped(me, j)
        pltpu.make_async_remote_copy(
            src_ref=v_ref,
            dst_ref=out_ref.at[peer],
            send_sem=send_sem.at[j],
            recv_sem=recv_sem.at[peer],
            device_id={"dom": peer},
            device_id_type=MESH,
        ).wait_recv()
    for copy in copies:
        copy.wait_send()


def circuit_kernel(v_ref, border_ref, term_ref, cur_ref, chg_ref, out_ref, volt, inc, flow):
    rows, nodes = v_ref.shape
    doms, _, border = border_ref.shape
    wide = inc.shape[0]
    elems = inc.shape[1]
    high, low = split(v_ref[...])
    volt[:rows, :nodes] = high
    volt[rows:, :nodes] = low
    for p in range(doms):
        high, low = split(border_ref[p])
        volt[:rows, nodes + p * border : nodes + (p + 1) * border] = high
        volt[rows:, nodes + p * border : nodes + (p + 1) * border] = low
    ew = 512
    kb = 256

    def gather(i, carry):
        cols = pl.ds(pl.multiple_of(i * ew, ew), ew)
        first = term_ref[0:1, cols]
        second = term_ref[1:2, cols]
        total = jnp.zeros((2 * rows, ew), jnp.float32)
        base = lax.broadcasted_iota(jnp.int32, (kb, ew), 0)
        for k in range(wide // kb):
            plus = jnp.where(base == first - k * kb, 1.0, 0.0)
            minus = jnp.where(base == second - k * kb, 1.0, 0.0)
            tile = (plus - minus).astype(jnp.bfloat16)
            inc[k * kb : (k + 1) * kb, cols] = tile
            total = total + dot(volt[:, k * kb : (k + 1) * kb], tile)
        across = total[:rows] + total[rows:]
        current = cur_ref[0:1, cols] * across + cur_ref[1:2, cols] * jnp.tanh(2.0 * across)
        charge = chg_ref[0:1, cols] * across + chg_ref[1:2, cols] * jnp.tanh(across)
        high, low = split(current)
        flow[:rows, cols] = high
        flow[rows : 2 * rows, cols] = low
        high, low = split(charge)
        flow[2 * rows : 3 * rows, cols] = high
        flow[3 * rows :, cols] = low
        return carry

    lax.fori_loop(0, elems // ew, gather, 0)

    def scatter(i, carry):
        mine = pl.ds(pl.multiple_of(i * kb, kb), kb)
        total = dot(flow[...], inc[mine, :], ((1,), (1,)))
        cur = total[:rows] + total[rows : 2 * rows]
        chg = total[2 * rows : 3 * rows] + total[3 * rows :]
        parts = []
        for c in range(kb // LANES):
            parts += [cur[:, c * LANES : (c + 1) * LANES], chg[:, c * LANES : (c + 1) * LANES]]
        out_ref[:, pl.ds(pl.multiple_of(i * 2 * kb, 2 * kb), 2 * kb)] = jnp.concatenate(parts, axis=1)
        return carry

    lax.fori_loop(0, wide // kb, scatter, 0)


def swap_pairs(x):
    even = lax.broadcasted_iota(jnp.int32, x.shape, 0) % 2 == 0
    rows = x.shape[0]
    return jnp.where(even, pltpu.roll(x, rows - 1, 0), pltpu.roll(x, 1, 0))


def newton_kernel(
    doms, freqs, entries,
    t_ref, high_ref, low_ref, src_ref, j0_ref, j1_ref,
    res_ref, step_ref, norm_ref,
    edge, summed, land, spec, back, part_dom, part_freq,
    edge_send, edge_recv, out_send, out_recv, back_send, back_recv,
    pd_send, pd_recv, pf_send, pf_recv, local_sem, local_sem2,
):
    dom = lax.axis_index("dom")
    freq = lax.axis_index("freq")
    rows, nodes = src_ref.shape
    chunks = nodes // freqs // LANES
    pair = 2 * LANES
    samples = rows * freqs
    barrier = pltpu.get_barrier_semaphore()
    for j in range(1, doms):
        pl.semaphore_signal(barrier, inc=1, device_id={"dom": flipped(dom, j)}, device_id_type=MESH)
    for j in range(1, freqs):
        pl.semaphore_signal(barrier, inc=1, device_id={"freq": flipped(freq, j)}, device_id_type=MESH)
    pl.semaphore_wait(barrier, doms + freqs - 2)

    def columns(block):
        return pl.ds(pl.multiple_of(block * pair, pair), pair)

    def edge_copy(j, owner, sender):
        return pltpu.make_async_remote_copy(
            src_ref=t_ref.at[:, columns(nodes // LANES + owner)],
            dst_ref=edge.at[sender],
            send_sem=edge_send.at[j],
            recv_sem=edge_recv.at[sender],
            device_id={"dom": flipped(dom, j)},
            device_id_type=MESH,
        )

    for j in range(1, doms):
        edge_copy(j, flipped(dom, j), dom).start()

    my_rows = pl.ds(pl.multiple_of(freq * rows, rows), rows)

    def out_copy(c, j, source, sender):
        return pltpu.make_async_remote_copy(
            src_ref=source,
            dst_ref=land.at[c, pl.ds(pl.multiple_of(sender * rows, rows), rows), :],
            send_sem=out_send.at[c, j],
            recv_sem=out_recv.at[c, sender],
            device_id={"freq": flipped(freq, j)},
            device_id_type=MESH,
        )

    def block_of(c, peer):
        return t_ref.at[:, columns(peer * chunks + c)]

    for c in range(chunks):
        for j in range(freqs - 1, 0, -1):
            peer = flipped(freq, j)
            if c == 0:
                @pl.when(peer != 0)
                def _():
                    out_copy(c, j, block_of(c, peer), freq).start()
            else:
                out_copy(c, j, block_of(c, peer), freq).start()

    for j in range(1, doms):
        edge_copy(j, dom, flipped(dom, j)).wait_recv()
    total = t_ref[:, :pair] + t_ref[:, columns(nodes // LANES + dom)]
    for p in range(doms):
        total = total + jnp.where(dom == p, 0.0, edge[p])
    summed[...] = total
    for j in range(freqs - 1, 0, -1):
        @pl.when(flipped(freq, j) == 0)
        def _():
            out_copy(0, j, summed, freq).start()

    for c in range(chunks):
        if c == 0:
            @pl.when(freq == 0)
            def _():
                land[0, my_rows, :] = total

            @pl.when(freq != 0)
            def _():
                land[0, my_rows, :] = t_ref[:, columns(freq * chunks)]
        else:
            land[c, my_rows, :] = t_ref[:, columns(freq * chunks + c)]

    def back_copy(c, j, target, sender):
        return pltpu.make_async_remote_copy(
            src_ref=spec.at[c, pl.ds(pl.multiple_of(target * rows, rows), rows), :],
            dst_ref=back.at[:, pl.ds(pl.multiple_of((sender * chunks + c) * LANES, LANES), LANES)],
            send_sem=back_send.at[c, j],
            recv_sem=back_recv.at[c, sender],
            device_id={"freq": flipped(freq, j)},
            device_id_type=MESH,
        )

    row = lax.broadcasted_iota(jnp.int32, (samples, LANES), 0)
    rate = (row // 2).astype(jnp.float32) * (2.0 / samples)
    rate = jnp.where(row % 2 == 0, rate, -rate)
    for c in range(chunks):
        for j in range(freqs - 1, 0, -1):
            peer = flipped(freq, j)
            out_copy(c, j, summed, peer).wait_recv()
        high, low = split(land[c])
        product = dot(high_ref[...], high) + (dot(high_ref[...], low) + dot(low_ref[...], high))
        spec[c] = product[:, :LANES] + rate * swap_pairs(product[:, LANES:])
        for j in range(freqs - 1, 0, -1):
            back_copy(c, j, flipped(freq, j), freq).start()
        back[:, pl.ds(pl.multiple_of((freq * chunks + c) * LANES, LANES), LANES)] = spec[c, my_rows, :]

    for c in range(chunks):
        for j in range(freqs - 1, 0, -1):
            peer = flipped(freq, j)
            back_copy(c, j, peer, peer).wait_recv()

    width = 2 * LANES
    raw_total = jnp.zeros((1, width), jnp.float32)
    res_total = jnp.zeros((1, width), jnp.float32)
    even = lax.broadcasted_iota(jnp.int32, (rows, width), 0) % 2 == 0
    for b in range(nodes // width):
        cols = slice(b * width, (b + 1) * width)
        residual = back[:, cols] - src_ref[:, cols]
        res_ref[:, cols] = residual
        upper = jnp.where(even, residual, pltpu.roll(residual, 1, 0))
        lower = jnp.where(even, pltpu.roll(residual, rows - 1, 0), residual)
        raw = -(j0_ref[:, cols] * upper + j1_ref[:, cols] * lower)
        step_ref[:, cols] = raw
        raw_total = raw_total + jnp.sum(raw * raw, axis=0, keepdims=True)
        res_total = res_total + jnp.sum(residual * residual, axis=0, keepdims=True)
    raw_sum = jnp.sum(raw_total, axis=1, keepdims=True)
    res_sum = jnp.sum(res_total, axis=1, keepdims=True)
    lane = lax.broadcasted_iota(jnp.int32, (8, LANES), 1)
    part_dom[dom] = jnp.where(lane == 0, raw_sum, jnp.where(lane == 1, res_sum, 0.0))

    def reduce_over(axis, count, me, part, send, recv):
        def copy_of(j, sender):
            return pltpu.make_async_remote_copy(
                src_ref=part.at[me],
                dst_ref=part.at[sender],
                send_sem=send.at[j],
                recv_sem=recv.at[sender],
                device_id={axis: flipped(me, j)},
                device_id_type=MESH,
            )

        for j in range(count - 1, 0, -1):
            copy_of(j, me).start()
        for j in range(count - 1, 0, -1):
            copy_of(j, flipped(me, j)).wait_recv()
        return sum((part[i] for i in range(1, count)), part[0])

    part_freq[freq] = reduce_over("dom", doms, dom, part_dom, pd_send, pd_recv)
    both = reduce_over("freq", freqs, freq, part_freq, pf_send, pf_recv)
    raw_sum = jnp.sum(jnp.where(lane == 0, both, 0.0)[:1], axis=1, keepdims=True)
    res_sum = jnp.sum(jnp.where(lane == 1, both, 0.0)[:1], axis=1, keepdims=True)
    spread = jnp.sqrt(raw_sum / entries + 1e-06)
    scale = jnp.minimum(1.0, trust_radius / spread)
    norm_ref[...] = jnp.broadcast_to(jnp.sqrt(res_sum), (8, LANES))
    for b in range(nodes // width):
        cols = slice(b * width, (b + 1) * width)
        step_ref[:, cols] = step_ref[:, cols] * scale

    for j in range(1, doms):
        edge_copy(j, flipped(dom, j), dom).wait_send()
    for c in range(chunks):
        for j in range(1, freqs):
            out_copy(c, j, summed, freq).wait_send()
            back_copy(c, j, flipped(freq, j), freq).wait_send()
    for axis, count, me, part, send, recv in (
        ("dom", doms, dom, part_dom, pd_send, pd_recv),
        ("freq", freqs, freq, part_freq, pf_send, pf_recv),
    ):
        for j in range(1, count):
            pltpu.make_async_remote_copy(
                src_ref=part.at[me],
                dst_ref=part.at[me],
                send_sem=send.at[j],
                recv_sem=recv.at[me],
                device_id={axis: flipped(me, j)},
                device_id_type=MESH,
            ).wait_send()


def body(doms, freqs, voltages, sources, terminals, elem_current, elem_charge, jacobi):
    rows, nodes = voltages.shape
    elems = terminals.shape[1]
    border = nodes // 16
    wide = nodes + doms * border
    samples = rows * freqs
    chunks = nodes // freqs // LANES
    f32, bf16 = jnp.float32, jnp.bfloat16
    dma = pltpu.SemaphoreType.DMA
    limit = 60 * 1024 * 1024
    vmem = pl.BlockSpec(memory_space=VMEM)
    edges = pl.pallas_call(
        functools.partial(border_kernel, doms),
        grid=(1,),
        out_shape=jax.ShapeDtypeStruct((doms, rows, border), f32),
        in_specs=[pl.BlockSpec((rows, border), lambda i: (0, 0))],
        out_specs=vmem,
        scratch_shapes=[dma((doms,)), dma((doms,)), dma(())],
        compiler_params=pltpu.CompilerParams(collective_id=0, has_side_effects=True),
    )(voltages)
    totals = pl.pallas_call(
        circuit_kernel,
        out_shape=jax.ShapeDtypeStruct((rows, 2 * wide), f32),
        in_specs=[vmem] * 5,
        out_specs=vmem,
        scratch_shapes=[
            VMEM((2 * rows, wide), bf16),
            VMEM((wide, elems), bf16),
            VMEM((4 * rows, elems), bf16),
        ],
        compiler_params=pltpu.CompilerParams(vmem_limit_bytes=limit),
    )(voltages, edges, terminals, elem_current, elem_charge)
    high, low = fourier_matrix(samples)
    residual, step, norm = pl.pallas_call(
        functools.partial(newton_kernel, doms, freqs, float(samples * nodes * doms)),
        out_shape=(
            jax.ShapeDtypeStruct((rows, nodes), f32),
            jax.ShapeDtypeStruct((rows, nodes), f32),
            jax.ShapeDtypeStruct((8, LANES), f32),
        ),
        in_specs=[vmem] * 6,
        out_specs=(vmem,) * 3,
        scratch_shapes=[
            VMEM((doms, rows, 2 * LANES), f32),
            VMEM((rows, 2 * LANES), f32),
            VMEM((chunks, samples, 2 * LANES), f32),
            VMEM((chunks, samples, LANES), f32),
            VMEM((rows, nodes), f32),
            VMEM((doms, 8, LANES), f32),
            VMEM((freqs, 8, LANES), f32),
            dma((doms,)), dma((doms,)),
            dma((chunks, freqs)), dma((chunks, freqs)),
            dma((chunks, freqs)), dma((chunks, freqs)),
            dma((doms,)), dma((doms,)),
            dma((freqs,)), dma((freqs,)),
            dma(()), dma(()),
        ],
        compiler_params=pltpu.CompilerParams(
            collective_id=1, has_side_effects=True, vmem_limit_bytes=limit
        ),
    )(
        totals, jnp.asarray(high), jnp.asarray(low), sources,
        jacobi[:, :, 0, :].reshape(rows, nodes), jacobi[:, :, 1, :].reshape(rows, nodes),
    )
    return residual, step, norm[0, 0]


def solution(mesh):
    placed = (
        P("freq", "dom"),
        P("freq", "dom"),
        P(None, "dom"),
        P(None, "dom"),
        P(None, "dom"),
        P("freq", None, None, "dom"),
    )
    return jax.shard_map(
        functools.partial(body, mesh.shape["dom"], mesh.shape["freq"]),
        mesh=mesh,
        in_specs=placed,
        out_specs=(P("freq", "dom"), P("freq", "dom"), P()),
        check_vma=False,
    )
```

```python
import functools
import math

import jax
import jax.numpy as jnp
import numpy as np
from jax import lax
from jax.experimental import pallas as pl
from jax.experimental.pallas import tpu as pltpu
from jax.sharding import PartitionSpec as P

MESH = pl.DeviceIdType.MESH
LANES = 128
VMEM = pltpu.VMEM
trust_radius = 2.0


def fourier_matrix(samples):
    row = np.arange(samples)
    harmonic = row // 2
    sine = row % 2 == 1
    order = np.where(harmonic == 0, np.where(sine, samples // 2, 0), harmonic)
    phase = (order[:, None] * np.arange(samples)[None, :] % samples) * (2.0 * math.pi / samples)
    values = np.where((sine & (harmonic > 0))[:, None], np.sin(phase), np.cos(phase))
    weight = np.where(harmonic == 0, math.sqrt(1.0 / samples), math.sqrt(2.0 / samples))
    full = (values * weight[:, None]).astype(np.float32)
    high = full.astype(jnp.bfloat16)
    low = (full - high.astype(np.float32)).astype(jnp.bfloat16)
    return high, low


def split(x):
    high = x.astype(jnp.bfloat16)
    low = (x - high.astype(jnp.float32)).astype(jnp.bfloat16)
    return high, low


def dot(a, b, contract=((1,), (0,))):
    return lax.dot_general(a, b, (contract, ((), ())), preferred_element_type=jnp.float32)


def xor(a, b, count):
    out, bit = 0, 1
    while bit < count:
        out = out + bit * ((a // bit + b // bit) % 2)
        bit *= 2
    return out


def swap_pairs(x):
    even = lax.broadcasted_iota(jnp.int32, x.shape, 0) % 2 == 0
    rows = x.shape[0]
    return jnp.where(even, pltpu.roll(x, rows - 1, 0), pltpu.roll(x, 1, 0))


def kernel(
    doms, freqs, entries,
    v_ref, term_ref, cur_ref, chg_ref, high_any, low_any, src_any, jac_any,
    back, raw_ref, norm_ref, scale_ref,
    volt, seen, inc, partial, flow, stage, edge_out, edge, land, spec, high_ref, low_ref, src_ref,
    jac_ref, part_dom, part_freq,
    v_send, v_recv, edge_send, edge_recv, out_send, out_recv, back_send, back_recv,
    pd_send, pd_recv, pf_send, pf_recv, load_sem,
):
    dom = lax.axis_index("dom")
    freq = lax.axis_index("freq")
    rows, nodes = v_ref.shape
    wide, elems = inc.shape
    border = seen.shape[2]
    samples = rows * freqs
    block = nodes // freqs
    chunks = block // LANES
    pair = 2 * LANES
    ew = 512
    kb = 256

    barrier = pltpu.get_barrier_semaphore()
    for j in range(1, doms):
        pl.semaphore_signal(barrier, inc=1, device_id={"dom": xor(dom, j, doms)}, device_id_type=MESH)
    for j in range(1, freqs):
        pl.semaphore_signal(barrier, inc=1, device_id={"freq": xor(freq, j, freqs)}, device_id_type=MESH)

    loads = [
        pltpu.make_async_copy(a, b, load_sem.at[i])
        for i, (a, b) in enumerate(
            ((high_any, high_ref), (low_any, low_ref), (src_any, src_ref), (jac_any, jac_ref))
        )
    ]
    for load in loads:
        load.start()

    def dom_copy(j, source, target, send, recv, sender):
        return pltpu.make_async_remote_copy(
            src_ref=source,
            dst_ref=target.at[sender],
            send_sem=send.at[j],
            recv_sem=recv.at[sender],
            device_id={"dom": xor(dom, j, doms)},
            device_id_type=MESH,
        )

    def v_copy(j, sender):
        return dom_copy(j, v_ref.at[:, :border], seen, v_send, v_recv, sender)

    def edge_copy(j, owner, sender):
        return dom_copy(j, edge_out.at[owner], edge, edge_send, edge_recv, sender)

    high, low = split(v_ref[...])
    volt[:rows, :nodes] = high
    volt[rows:, :nodes] = low

    def build(i, carry):
        @pl.when(i == 1)
        def _():
            pl.semaphore_wait(barrier, doms + freqs - 2)
            for j in range(doms - 1, 0, -1):
                v_copy(j, dom).start()

        cols = pl.ds(pl.multiple_of(i * ew, ew), ew)
        first = term_ref[0:1, cols]
        second = term_ref[1:2, cols]
        same = first == second
        first = jnp.where(same, -1, first)
        second = jnp.where(same, -1, second)
        total = jnp.zeros((2 * rows, ew), jnp.float32)
        base = lax.broadcasted_iota(jnp.int32, (kb, ew), 0)
        for k in range(wide // kb):
            tile = jnp.where(base == first - k * kb, 1.0, jnp.where(base == second - k * kb, -1.0, 0.0))
            tile = tile.astype(jnp.bfloat16)
            inc[k * kb : (k + 1) * kb, cols] = tile
            if k * kb < nodes:
                total = total + dot(volt[:, k * kb : (k + 1) * kb], tile)
        partial[:, cols] = total[:rows] + total[rows:]
        return carry

    lax.fori_loop(0, elems // ew, build, 0)

    seen[dom] = v_ref[:, :border]
    for j in range(1, doms):
        v_copy(j, xor(dom, j, doms)).wait_recv()
    for p in range(doms):
        high, low = split(seen[p])
        volt[:rows, nodes + p * border : nodes + (p + 1) * border] = high
        volt[rows:, nodes + p * border : nodes + (p + 1) * border] = low

    def evaluate(i, carry):
        cols = pl.ds(pl.multiple_of(i * ew, ew), ew)
        total = dot(volt[:, nodes:], inc[nodes:, cols])
        across = partial[:, cols] + (total[:rows] + total[rows:])
        current = cur_ref[0:1, cols] * across + cur_ref[1:2, cols] * jnp.tanh(2.0 * across)
        charge = chg_ref[0:1, cols] * across + chg_ref[1:2, cols] * jnp.tanh(across)
        high, low = split(current)
        flow[:rows, cols] = high
        flow[rows : 2 * rows, cols] = low
        high, low = split(charge)
        flow[2 * rows : 3 * rows, cols] = high
        flow[3 * rows :, cols] = low
        return carry

    lax.fori_loop(0, elems // ew, evaluate, 0)

    def scatter(start, width):
        total = dot(flow[...], inc[pl.ds(pl.multiple_of(start, LANES), width), :], ((1,), (1,)))
        cur = total[:rows] + total[rows : 2 * rows]
        chg = total[2 * rows : 3 * rows] + total[3 * rows :]
        return [
            jnp.concatenate([cur[:, c * LANES : (c + 1) * LANES], chg[:, c * LANES : (c + 1) * LANES]], axis=1)
            for c in range(width // LANES)
        ]

    per = kb // LANES

    def border_block(i, carry):
        pieces = scatter(nodes + i * kb, kb)
        for c in range(per):
            edge_out[i * per + c] = pieces[c]
        return carry

    lax.fori_loop(0, (wide - nodes) // kb, border_block, 0)
    for j in range(doms - 1, 0, -1):
        edge_copy(j, xor(dom, j, doms), dom).start()

    my_rows = pl.ds(pl.multiple_of(freq * rows, rows), rows)

    def out_copy(c, j, sender):
        peer = xor(freq, j, freqs)
        return pltpu.make_async_remote_copy(
            src_ref=stage.at[c, peer],
            dst_ref=land.at[c, pl.ds(pl.multiple_of(sender * rows, rows), rows), :],
            send_sem=out_send.at[c, j],
            recv_sem=out_recv.at[c, sender],
            device_id={"freq": peer},
            device_id_type=MESH,
        )

    def node_block(i, carry):
        j = freqs - 1 - i
        peer = xor(freq, j, freqs)
        pieces = scatter(peer * block, block)
        for c in range(chunks):
            stage[c, peer] = pieces[c]

        @pl.when(peer == 0)
        def _():
            for k in range(1, doms):
                edge_copy(k, dom, xor(dom, k, doms)).wait_recv()
            total = stage[0, 0] + edge_out[dom]
            for p in range(doms):
                total = total + jnp.where(dom == p, 0.0, edge[p])
            stage[0, 0] = total

        @pl.when(j != 0)
        def _():
            out_copy(0, j, freq).start()

        return carry

    lax.fori_loop(0, freqs, node_block, 0)

    def later(i, carry):
        for c in range(1, chunks):
            out_copy(c, freqs - 1 - i, freq).start()
        return carry

    if chunks > 1:
        lax.fori_loop(0, freqs - 1, later, 0)

    for c in range(chunks):
        land[c, my_rows, :] = stage[c, freq]

    def back_columns(c, sender):
        return pl.ds(pl.multiple_of((sender * chunks + c) * LANES, LANES), LANES)

    def back_copy(c, j, target, sender):
        return pltpu.make_async_remote_copy(
            src_ref=spec.at[c, pl.ds(pl.multiple_of(target * rows, rows), rows), :],
            dst_ref=back.at[:, back_columns(c, sender)],
            send_sem=back_send.at[c, j],
            recv_sem=back_recv.at[c, sender],
            device_id={"freq": xor(freq, j, freqs)},
            device_id_type=MESH,
        )

    for load in loads:
        load.wait()
    row = lax.broadcasted_iota(jnp.int32, (samples, LANES), 0)
    rate = (row // 2).astype(jnp.float32) * (2.0 / samples)
    rate = jnp.where(row % 2 == 0, rate, -rate)
    for c in range(chunks):
        def arrived(i, carry):
            out_copy(c, freqs - 1 - i, xor(freq, freqs - 1 - i, freqs)).wait_recv()
            return carry

        lax.fori_loop(0, freqs - 1, arrived, 0)
        high, low = split(land[c])
        product = dot(high_ref[...], high) + (dot(high_ref[...], low) + dot(low_ref[...], high))
        spec[c] = product[:, :LANES] + rate * swap_pairs(product[:, LANES:])

        def give(i, carry):
            j = freqs - 1 - i
            back_copy(c, j, xor(freq, j, freqs), freq).start()
            return carry

        lax.fori_loop(0, freqs - 1, give, 0)
        back[:, back_columns(c, freq)] = spec[c, my_rows, :]

    even = lax.broadcasted_iota(jnp.int32, (rows, LANES), 0) % 2 == 0
    sums = (jnp.zeros((8, LANES), jnp.float32), jnp.zeros((8, LANES), jnp.float32))

    def fold(x):
        return jnp.sum((x * x).reshape(rows // 8, 8, LANES), axis=0)

    for c in range(chunks):
        def finish(j, carry):
            peer = xor(freq, j, freqs)

            @pl.when(j != 0)
            def _():
                back_copy(c, j, peer, peer).wait_recv()

            cols = back_columns(c, peer)
            residual = back[:, cols] - src_ref[:, cols]
            upper = jnp.where(even, residual, pltpu.roll(residual, 1, 0))
            lower = jnp.where(even, pltpu.roll(residual, rows - 1, 0), residual)
            raw = -(jac_ref[:, 0, cols] * upper + jac_ref[:, 1, cols] * lower)
            raw_ref[:, cols] = raw
            return carry[0] + fold(raw), carry[1] + fold(residual)

        sums = lax.fori_loop(0, freqs, finish, sums)

    def whole(x):
        return jnp.sum(jnp.sum(x, axis=0, keepdims=True), axis=1, keepdims=True)

    lane = lax.broadcasted_iota(jnp.int32, (8, LANES), 1)
    part_dom[dom] = jnp.where(lane == 0, whole(sums[0]), jnp.where(lane == 1, whole(sums[1]), 0.0))

    def part_copy(axis, count, me, part, send, recv, j, sender):
        return pltpu.make_async_remote_copy(
            src_ref=part.at[me],
            dst_ref=part.at[sender],
            send_sem=send.at[j],
            recv_sem=recv.at[sender],
            device_id={axis: xor(me, j, count)},
            device_id_type=MESH,
        )

    def reduce_over(axis, count, me, part, send, recv):
        for j in range(count - 1, 0, -1):
            part_copy(axis, count, me, part, send, recv, j, me).start()
        for j in range(count - 1, 0, -1):
            part_copy(axis, count, me, part, send, recv, j, xor(me, j, count)).wait_recv()
        return sum((part[i] for i in range(1, count)), part[0])

    part_freq[freq] = reduce_over("dom", doms, dom, part_dom, pd_send, pd_recv)
    both = reduce_over("freq", freqs, freq, part_freq, pf_send, pf_recv)
    raw_sum = jnp.sum(jnp.where(lane == 0, both, 0.0)[:1], axis=1, keepdims=True)
    res_sum = jnp.sum(jnp.where(lane == 1, both, 0.0)[:1], axis=1, keepdims=True)
    spread = jnp.sqrt(raw_sum / entries + 1e-06)
    scale_ref[...] = jnp.minimum(1.0, trust_radius / spread)
    norm_ref[...] = jnp.sqrt(res_sum)

    for j in range(1, doms):
        v_copy(j, dom).wait_send()
        edge_copy(j, dom, dom).wait_send()
        part_copy("dom", doms, dom, part_dom, pd_send, pd_recv, j, dom).wait_send()

    def drain(i, carry):
        j = i + 1
        for c in range(chunks):
            out_copy(c, j, freq).wait_send()
            back_copy(c, j, freq, freq).wait_send()
        part_copy("freq", freqs, freq, part_freq, pf_send, pf_recv, j, freq).wait_send()
        return carry

    lax.fori_loop(0, freqs - 1, drain, 0)


def body(doms, freqs, voltages, sources, terminals, elem_current, elem_charge, jacobi):
    rows, nodes = voltages.shape
    elems = terminals.shape[1]
    border = nodes // 16
    wide = nodes + doms * border
    samples = rows * freqs
    chunks = nodes // freqs // LANES
    f32, bf16 = jnp.float32, jnp.bfloat16
    dma = pltpu.SemaphoreType.DMA
    vmem = pl.BlockSpec(memory_space=VMEM)
    anywhere = pl.BlockSpec(memory_space=pl.ANY)
    high, low = fourier_matrix(samples)
    back, raw, norm, scale = pl.pallas_call(
        functools.partial(kernel, doms, freqs, float(samples * nodes * doms)),
        out_shape=(
            jax.ShapeDtypeStruct((rows, nodes), f32),
            jax.ShapeDtypeStruct((rows, nodes), f32),
            jax.ShapeDtypeStruct((1, 1), f32),
            jax.ShapeDtypeStruct((1, 1), f32),
        ),
        in_specs=[vmem] * 4 + [anywhere] * 4,
        out_specs=(vmem,) * 4,
        scratch_shapes=[
            VMEM((2 * rows, wide), bf16),
            VMEM((doms, rows, border), f32),
            VMEM((wide, elems), bf16),
            VMEM((rows, elems), f32),
            VMEM((4 * rows, elems), bf16),
            VMEM((chunks, freqs, rows, 2 * LANES), f32),
            VMEM((doms, rows, 2 * LANES), f32),
            VMEM((doms, rows, 2 * LANES), f32),
            VMEM((chunks, samples, 2 * LANES), f32),
            VMEM((chunks, samples, LANES), f32),
            VMEM((samples, samples), bf16),
            VMEM((samples, samples), bf16),
            VMEM((rows, nodes), f32),
            VMEM((rows, 2, nodes), f32),
            VMEM((doms, 8, LANES), f32),
            VMEM((freqs, 8, LANES), f32),
            dma((doms,)), dma((doms,)),
            dma((doms,)), dma((doms,)),
            dma((chunks, freqs)), dma((chunks, freqs)),
            dma((chunks, freqs)), dma((chunks, freqs)),
            dma((doms,)), dma((doms,)),
            dma((freqs,)), dma((freqs,)),
            dma((4,)),
        ],
        compiler_params=pltpu.CompilerParams(
            collective_id=0, has_side_effects=True, vmem_limit_bytes=60 * 1024 * 1024
        ),
    )(
        voltages, terminals, elem_current, elem_charge,
        jnp.asarray(high), jnp.asarray(low), sources, jacobi.reshape(rows, 2, nodes),
    )
    return back - sources, raw * scale, norm.reshape(())


def solution(mesh):
    placed = (
        P("freq", "dom"),
        P("freq", "dom"),
        P(None, "dom"),
        P(None, "dom"),
        P(None, "dom"),
        P("freq", None, None, "dom"),
    )
    return jax.shard_map(
        functools.partial(body, mesh.shape["dom"], mesh.shape["freq"]),
        mesh=mesh,
        in_specs=placed,
        out_specs=(P("freq", "dom"), P("freq", "dom"), P()),
        check_vma=False,
    )
```

```python
import functools
import math

import jax
import jax.numpy as jnp
import numpy as np
from jax import lax
from jax.experimental import pallas as pl
from jax.experimental.pallas import tpu as pltpu
from jax.sharding import PartitionSpec as P

MESH = pl.DeviceIdType.MESH
LANES = 128
VMEM = pltpu.VMEM
trust_radius = 2.0


def fourier_matrix(samples):
    row = np.arange(samples)
    harmonic = row // 2
    sine = row % 2 == 1
    order = np.where(harmonic == 0, np.where(sine, samples // 2, 0), harmonic)
    phase = (order[:, None] * np.arange(samples)[None, :] % samples) * (2.0 * math.pi / samples)
    values = np.where((sine & (harmonic > 0))[:, None], np.sin(phase), np.cos(phase))
    weight = np.where(harmonic == 0, math.sqrt(1.0 / samples), math.sqrt(2.0 / samples))
    full = (values * weight[:, None]).astype(np.float32)
    high = full.astype(jnp.bfloat16)
    low = (full - high.astype(np.float32)).astype(jnp.bfloat16)
    return high, low


def split(x):
    high = x.astype(jnp.bfloat16)
    low = (x - high.astype(jnp.float32)).astype(jnp.bfloat16)
    return high, low


def dot(a, b, contract=((1,), (0,))):
    return lax.dot_general(a, b, (contract, ((), ())), preferred_element_type=jnp.float32)


def xor(a, b, count):
    out, bit = 0, 1
    while bit < count:
        out = out + bit * ((a // bit + b // bit) % 2)
        bit *= 2
    return out


def swap_pairs(x):
    even = lax.broadcasted_iota(jnp.int32, x.shape, 0) % 2 == 0
    rows = x.shape[0]
    return jnp.where(even, pltpu.roll(x, rows - 1, 0), pltpu.roll(x, 1, 0))


def kernel(
    doms, freqs, entries,
    v_ref, term_ref, cur_ref, chg_ref, high_any, low_any, src_any, jac_any,
    out_any, norm_ref, scale_ref,
    back, raw_ref, volt, seen, inc, partial, flow, stage, edge_out, edge, land, spec, high_ref, low_ref, src_ref,
    jac_ref, part_dom, part_freq,
    v_send, v_recv, edge_send, edge_recv, out_send, out_recv, back_send, back_recv,
    pd_send, pd_recv, pf_send, pf_recv, load_sem, store_sem,
):
    dom = lax.axis_index("dom")
    freq = lax.axis_index("freq")
    rows, nodes = v_ref.shape
    wide, elems = inc.shape
    border = seen.shape[2]
    samples = rows * freqs
    block = nodes // freqs
    chunks = block // LANES
    pair = 2 * LANES
    ew = 512
    kb = 256
    one, zero = jnp.bfloat16(1.0), jnp.bfloat16(0.0)

    barrier = pltpu.get_barrier_semaphore()
    for j in range(1, doms):
        pl.semaphore_signal(barrier, inc=1, device_id={"dom": xor(dom, j, doms)}, device_id_type=MESH)
    for j in range(1, freqs):
        pl.semaphore_signal(barrier, inc=1, device_id={"freq": xor(freq, j, freqs)}, device_id_type=MESH)

    loads = [
        pltpu.make_async_copy(a, b, load_sem.at[i])
        for i, (a, b) in enumerate(
            ((high_any, high_ref), (low_any, low_ref), (src_any, src_ref), (jac_any, jac_ref))
        )
    ]
    for load in loads:
        load.start()

    def dom_copy(j, source, target, send, recv, sender):
        return pltpu.make_async_remote_copy(
            src_ref=source,
            dst_ref=target.at[sender],
            send_sem=send.at[j],
            recv_sem=recv.at[sender],
            device_id={"dom": xor(dom, j, doms)},
            device_id_type=MESH,
        )

    def v_copy(j, sender):
        return dom_copy(j, v_ref.at[:, :border], seen, v_send, v_recv, sender)

    def edge_copy(j, owner, sender):
        return dom_copy(j, edge_out.at[owner], edge, edge_send, edge_recv, sender)

    high, low = split(v_ref[...])
    volt[:rows, :nodes] = high
    volt[rows:, :nodes] = low

    def build(i, carry):
        @pl.when(i == 1)
        def _():
            pl.semaphore_wait(barrier, doms + freqs - 2)
            for j in range(doms - 1, 0, -1):
                v_copy(j, dom).start()

        cols = pl.ds(pl.multiple_of(i * ew, ew), ew)
        first = term_ref[0:1, cols]
        second = term_ref[1:2, cols]
        same = first == second
        first = jnp.where(same, -1, first)
        second = jnp.where(same, -1, second)
        total = jnp.zeros((2 * rows, ew), jnp.float32)
        base = lax.broadcasted_iota(jnp.int16, (kb, ew), 0)
        for k in range(wide // kb):
            plus = base == (first - k * kb).astype(jnp.int16)
            minus = base == (second - k * kb).astype(jnp.int16)
            tile = jnp.where(plus, one, jnp.where(minus, -one, zero))
            inc[k * kb : (k + 1) * kb, cols] = tile
            if k * kb < nodes:
                total = total + dot(volt[:, k * kb : (k + 1) * kb], tile)
        partial[:, cols] = total[:rows] + total[rows:]
        return carry

    lax.fori_loop(0, elems // ew, build, 0)

    seen[dom] = v_ref[:, :border]
    for j in range(1, doms):
        v_copy(j, xor(dom, j, doms)).wait_recv()
    for p in range(doms):
        high, low = split(seen[p])
        volt[:rows, nodes + p * border : nodes + (p + 1) * border] = high
        volt[rows:, nodes + p * border : nodes + (p + 1) * border] = low

    def evaluate(i, carry):
        cols = pl.ds(pl.multiple_of(i * ew, ew), ew)
        total = dot(volt[:, nodes:], inc[nodes:, cols])
        across = partial[:, cols] + (total[:rows] + total[rows:])
        current = cur_ref[0:1, cols] * across + cur_ref[1:2, cols] * jnp.tanh(2.0 * across)
        charge = chg_ref[0:1, cols] * across + chg_ref[1:2, cols] * jnp.tanh(across)
        high, low = split(current)
        flow[:rows, cols] = high
        flow[rows : 2 * rows, cols] = low
        high, low = split(charge)
        flow[2 * rows : 3 * rows, cols] = high
        flow[3 * rows :, cols] = low
        return carry

    lax.fori_loop(0, elems // ew, evaluate, 0)

    def scatter(start, width):
        total = dot(flow[...], inc[pl.ds(pl.multiple_of(start, LANES), width), :], ((1,), (1,)))
        cur = total[:rows] + total[rows : 2 * rows]
        chg = total[2 * rows : 3 * rows] + total[3 * rows :]
        return [
            jnp.concatenate([cur[:, c * LANES : (c + 1) * LANES], chg[:, c * LANES : (c + 1) * LANES]], axis=1)
            for c in range(width // LANES)
        ]

    per = kb // LANES

    def border_block(i, carry):
        pieces = scatter(nodes + i * kb, kb)
        for c in range(per):
            edge_out[i * per + c] = pieces[c]
        return carry

    my_rows = pl.ds(pl.multiple_of(freq * rows, rows), rows)

    def out_copy(c, j, sender):
        peer = xor(freq, j, freqs)
        return pltpu.make_async_remote_copy(
            src_ref=stage.at[c, peer],
            dst_ref=land.at[c, pl.ds(pl.multiple_of(sender * rows, rows), rows), :],
            send_sem=out_send.at[c, j],
            recv_sem=out_recv.at[c, sender],
            device_id={"freq": peer},
            device_id_type=MESH,
        )

    def node_block(i, carry):
        half = freqs // 2
        far = (1 - freq // half) * half + half - 1 - i
        peer = jnp.where(i < half, far, xor(freq, freqs - 1 - i, freqs))
        j = xor(freq, peer, freqs)

        @pl.when(i == 1)
        def _():
            lax.fori_loop(0, (wide - nodes) // kb, border_block, 0)
            for k in range(doms - 1, 0, -1):
                edge_copy(k, xor(dom, k, doms), dom).start()

        pieces = scatter(peer * block, block)
        for c in range(chunks):
            stage[c, peer] = pieces[c]

        @pl.when(peer == 0)
        def _():
            for k in range(1, doms):
                edge_copy(k, dom, xor(dom, k, doms)).wait_recv()
            total = stage[0, 0] + edge_out[dom]
            for p in range(doms):
                total = total + jnp.where(dom == p, 0.0, edge[p])
            stage[0, 0] = total

        @pl.when(j != 0)
        def _():
            out_copy(0, j, freq).start()

        return carry

    lax.fori_loop(0, freqs, node_block, 0)

    def later(i, carry):
        for c in range(1, chunks):
            out_copy(c, freqs - 1 - i, freq).start()
        return carry

    if chunks > 1:
        lax.fori_loop(0, freqs - 1, later, 0)

    for c in range(chunks):
        land[c, my_rows, :] = stage[c, freq]

    def back_columns(c, sender):
        return pl.ds(pl.multiple_of((sender * chunks + c) * LANES, LANES), LANES)

    def back_copy(c, j, target, sender):
        return pltpu.make_async_remote_copy(
            src_ref=spec.at[c, pl.ds(pl.multiple_of(target * rows, rows), rows), :],
            dst_ref=back.at[:, back_columns(c, sender)],
            send_sem=back_send.at[c, j],
            recv_sem=back_recv.at[c, sender],
            device_id={"freq": xor(freq, j, freqs)},
            device_id_type=MESH,
        )

    for load in loads:
        load.wait()
    row = lax.broadcasted_iota(jnp.int32, (samples, LANES), 0)
    rate = (row // 2).astype(jnp.float32) * (2.0 / samples)
    rate = jnp.where(row % 2 == 0, rate, -rate)
    for c in range(chunks):
        def arrived(i, carry):
            out_copy(c, freqs - 1 - i, xor(freq, freqs - 1 - i, freqs)).wait_recv()
            return carry

        lax.fori_loop(0, freqs - 1, arrived, 0)
        high, low = split(land[c])
        product = dot(high_ref[...], high) + (dot(high_ref[...], low) + dot(low_ref[...], high))
        spec[c] = product[:, :LANES] + rate * swap_pairs(product[:, LANES:])

        def give(i, carry):
            j = freqs - 1 - i
            back_copy(c, j, xor(freq, j, freqs), freq).start()
            return carry

        lax.fori_loop(0, freqs - 1, give, 0)
        back[:, back_columns(c, freq)] = spec[c, my_rows, :]

    even = lax.broadcasted_iota(jnp.int32, (rows, LANES), 0) % 2 == 0
    sums = (jnp.zeros((8, LANES), jnp.float32), jnp.zeros((8, LANES), jnp.float32))

    def fold(x):
        return jnp.sum((x * x).reshape(rows // 8, 8, LANES), axis=0)

    for c in range(chunks):
        def finish(j, carry):
            peer = xor(freq, j, freqs)

            @pl.when(j != 0)
            def _():
                back_copy(c, j, peer, peer).wait_recv()

            cols = back_columns(c, peer)
            residual = back[:, cols] - src_ref[:, cols]
            upper = jnp.where(even, residual, pltpu.roll(residual, 1, 0))
            lower = jnp.where(even, pltpu.roll(residual, rows - 1, 0), residual)
            raw = -(jac_ref[:, 0, cols] * upper + jac_ref[:, 1, cols] * lower)
            back[:, cols] = residual
            raw_ref[:, cols] = raw
            return carry[0] + fold(raw), carry[1] + fold(residual)

        sums = lax.fori_loop(0, freqs, finish, sums)

    stores = [
        pltpu.make_async_copy(a, out_any.at[i], store_sem.at[i]) for i, a in enumerate((back, raw_ref))
    ]
    for store in stores:
        store.start()

    def whole(x):
        return jnp.sum(jnp.sum(x, axis=0, keepdims=True), axis=1, keepdims=True)

    lane = lax.broadcasted_iota(jnp.int32, (8, LANES), 1)
    part_dom[dom] = jnp.where(lane == 0, whole(sums[0]), jnp.where(lane == 1, whole(sums[1]), 0.0))

    def part_copy(axis, count, me, part, send, recv, j, sender):
        return pltpu.make_async_remote_copy(
            src_ref=part.at[me],
            dst_ref=part.at[sender],
            send_sem=send.at[j],
            recv_sem=recv.at[sender],
            device_id={axis: xor(me, j, count)},
            device_id_type=MESH,
        )

    def reduce_over(axis, count, me, part, send, recv):
        for j in range(count - 1, 0, -1):
            part_copy(axis, count, me, part, send, recv, j, me).start()
        for j in range(count - 1, 0, -1):
            part_copy(axis, count, me, part, send, recv, j, xor(me, j, count)).wait_recv()
        return sum((part[i] for i in range(1, count)), part[0])

    part_freq[freq] = reduce_over("dom", doms, dom, part_dom, pd_send, pd_recv)
    both = reduce_over("freq", freqs, freq, part_freq, pf_send, pf_recv)
    raw_sum = jnp.sum(jnp.where(lane == 0, both, 0.0)[:1], axis=1, keepdims=True)
    res_sum = jnp.sum(jnp.where(lane == 1, both, 0.0)[:1], axis=1, keepdims=True)
    spread = jnp.sqrt(raw_sum / entries + 1e-06)
    scale_ref[...] = jnp.minimum(1.0, trust_radius / spread)
    norm_ref[...] = jnp.sqrt(res_sum)
    for store in stores:
        store.wait()

    for j in range(1, doms):
        v_copy(j, dom).wait_send()
        edge_copy(j, dom, dom).wait_send()
        part_copy("dom", doms, dom, part_dom, pd_send, pd_recv, j, dom).wait_send()

    def drain(i, carry):
        j = i + 1
        for c in range(chunks):
            out_copy(c, j, freq).wait_send()
            back_copy(c, j, freq, freq).wait_send()
        part_copy("freq", freqs, freq, part_freq, pf_send, pf_recv, j, freq).wait_send()
        return carry

    lax.fori_loop(0, freqs - 1, drain, 0)


def damp_kernel(both_ref, scale_ref, residual_ref, step_ref):
    residual_ref[...] = both_ref[0]
    step_ref[...] = both_ref[1] * scale_ref[...]


def body(doms, freqs, voltages, sources, terminals, elem_current, elem_charge, jacobi):
    rows, nodes = voltages.shape
    elems = terminals.shape[1]
    border = nodes // 16
    wide = nodes + doms * border
    samples = rows * freqs
    chunks = nodes // freqs // LANES
    f32, bf16 = jnp.float32, jnp.bfloat16
    dma = pltpu.SemaphoreType.DMA
    vmem = pl.BlockSpec(memory_space=VMEM)
    anywhere = pl.BlockSpec(memory_space=pl.ANY)
    high, low = fourier_matrix(samples)
    both, norm, scale = pl.pallas_call(
        functools.partial(kernel, doms, freqs, float(samples * nodes * doms)),
        out_shape=(
            jax.ShapeDtypeStruct((2, rows, nodes), f32),
            jax.ShapeDtypeStruct((1, 1), f32),
            jax.ShapeDtypeStruct((1, 1), f32),
        ),
        in_specs=[vmem] * 4 + [anywhere] * 4,
        out_specs=(anywhere, vmem, vmem),
        scratch_shapes=[
            VMEM((rows, nodes), f32),
            VMEM((rows, nodes), f32),
            VMEM((2 * rows, wide), bf16),
            VMEM((doms, rows, border), f32),
            VMEM((wide, elems), bf16),
            VMEM((rows, elems), f32),
            VMEM((4 * rows, elems), bf16),
            VMEM((chunks, freqs, rows, 2 * LANES), f32),
            VMEM((doms, rows, 2 * LANES), f32),
            VMEM((doms, rows, 2 * LANES), f32),
            VMEM((chunks, samples, 2 * LANES), f32),
            VMEM((chunks, samples, LANES), f32),
            VMEM((samples, samples), bf16),
            VMEM((samples, samples), bf16),
            VMEM((rows, nodes), f32),
            VMEM((rows, 2, nodes), f32),
            VMEM((doms, 8, LANES), f32),
            VMEM((freqs, 8, LANES), f32),
            dma((doms,)), dma((doms,)),
            dma((doms,)), dma((doms,)),
            dma((chunks, freqs)), dma((chunks, freqs)),
            dma((chunks, freqs)), dma((chunks, freqs)),
            dma((doms,)), dma((doms,)),
            dma((freqs,)), dma((freqs,)),
            dma((4,)),
            dma((2,)),
        ],
        compiler_params=pltpu.CompilerParams(
            collective_id=0, has_side_effects=True, vmem_limit_bytes=60 * 1024 * 1024
        ),
    )(
        voltages, terminals, elem_current, elem_charge,
        jnp.asarray(high), jnp.asarray(low), sources, jacobi.reshape(rows, 2, nodes),
    )
    part = pl.BlockSpec((rows // 2, nodes), lambda i: (i, 0))
    residual, step = pl.pallas_call(
        damp_kernel,
        grid=(2,),
        out_shape=(jax.ShapeDtypeStruct((rows, nodes), f32),) * 2,
        in_specs=[
            pl.BlockSpec((2, rows // 2, nodes), lambda i: (0, i, 0)),
            pl.BlockSpec((1, 1), lambda i: (0, 0)),
        ],
        out_specs=(part, part),
    )(both, scale)
    return residual, step, norm.reshape(())


def solution(mesh):
    placed = (
        P("freq", "dom"),
        P("freq", "dom"),
        P(None, "dom"),
        P(None, "dom"),
        P(None, "dom"),
        P("freq", None, None, "dom"),
    )
    return jax.shard_map(
        functools.partial(body, mesh.shape["dom"], mesh.shape["freq"]),
        mesh=mesh,
        in_specs=placed,
        out_specs=(P("freq", "dom"), P("freq", "dom"), P()),
        check_vma=False,
    )
```

```python
import functools
import math

import jax
import jax.numpy as jnp
import numpy as np
from jax import lax
from jax.experimental import pallas as pl
from jax.experimental.pallas import tpu as pltpu
from jax.sharding import PartitionSpec as P

MESH = pl.DeviceIdType.MESH
LANES = 128
VMEM = pltpu.VMEM
trust_radius = 2.0


def fourier_matrix(samples):
    row = np.arange(samples)
    harmonic = row // 2
    sine = row % 2 == 1
    order = np.where(harmonic == 0, np.where(sine, samples // 2, 0), harmonic)
    phase = (order[:, None] * np.arange(samples)[None, :] % samples) * (2.0 * math.pi / samples)
    values = np.where((sine & (harmonic > 0))[:, None], np.sin(phase), np.cos(phase))
    weight = np.where(harmonic == 0, math.sqrt(1.0 / samples), math.sqrt(2.0 / samples))
    full = (values * weight[:, None]).astype(np.float32)
    high = full.astype(jnp.bfloat16)
    low = (full - high.astype(np.float32)).astype(jnp.bfloat16)
    return high, low


def split(x):
    high = x.astype(jnp.bfloat16)
    low = (x - high.astype(jnp.float32)).astype(jnp.bfloat16)
    return high, low


def dot(a, b, contract=((1,), (0,))):
    return lax.dot_general(a, b, (contract, ((), ())), preferred_element_type=jnp.float32)


def xor(a, b, count):
    out, bit = 0, 1
    while bit < count:
        out = out + bit * ((a // bit + b // bit) % 2)
        bit *= 2
    return out


def swap_pairs(x):
    even = lax.broadcasted_iota(jnp.int32, x.shape, 0) % 2 == 0
    rows = x.shape[0]
    return jnp.where(even, pltpu.roll(x, rows - 1, 0), pltpu.roll(x, 1, 0))


def kernel(
    doms, freqs, entries,
    v_ref, term_ref, cur_ref, chg_ref, high_any, low_any, src_any, jac_any,
    out_any, norm_ref, scale_ref,
    back, raw_ref, volt, seen, inc, partial, flow, stage, edge_out, edge, land, spec, mirror, joined, high_ref, low_ref, src_ref,
    jac_ref, part_dom, part_freq,
    v_send, v_recv, edge_send, edge_recv, out_send, out_recv, mirror_send, mirror_recv, back_send, back_recv,
    pd_send, pd_recv, pf_send, pf_recv, load_sem, store_sem,
):
    dom = lax.axis_index("dom")
    freq = lax.axis_index("freq")
    rows, nodes = v_ref.shape
    wide, elems = inc.shape
    border = seen.shape[2]
    samples = rows * freqs
    near = freqs // 2
    half = freq // near
    mine = freq % near
    mirror_id = freq + near * (1 - 2 * half)
    group = nodes // near
    chunks = group // LANES
    ew = 512
    kb = 256
    one, zero = jnp.bfloat16(1.0), jnp.bfloat16(0.0)

    barrier = pltpu.get_barrier_semaphore()
    for j in range(1, doms):
        pl.semaphore_signal(barrier, inc=1, device_id={"dom": xor(dom, j, doms)}, device_id_type=MESH)
    for j in range(1, freqs):
        pl.semaphore_signal(barrier, inc=1, device_id={"freq": xor(freq, j, freqs)}, device_id_type=MESH)

    loads = [
        pltpu.make_async_copy(a, b, load_sem.at[i])
        for i, (a, b) in enumerate(
            ((high_any, high_ref), (low_any, low_ref), (src_any, src_ref), (jac_any, jac_ref))
        )
    ]
    for load in loads:
        load.start()

    def dom_copy(j, source, target, send, recv, sender):
        return pltpu.make_async_remote_copy(
            src_ref=source,
            dst_ref=target.at[sender],
            send_sem=send.at[j],
            recv_sem=recv.at[sender],
            device_id={"dom": xor(dom, j, doms)},
            device_id_type=MESH,
        )

    def v_copy(j, sender):
        return dom_copy(j, v_ref.at[:, :border], seen, v_send, v_recv, sender)

    def edge_copy(j, owner, sender):
        return dom_copy(j, edge_out.at[owner], edge, edge_send, edge_recv, sender)

    high, low = split(v_ref[...])
    volt[:rows, :nodes] = high
    volt[rows:, :nodes] = low

    def build(i, carry):
        @pl.when(i == 1)
        def _():
            pl.semaphore_wait(barrier, doms + freqs - 2)
            for j in range(doms - 1, 0, -1):
                v_copy(j, dom).start()

        cols = pl.ds(pl.multiple_of(i * ew, ew), ew)
        first = term_ref[0:1, cols]
        second = term_ref[1:2, cols]
        same = first == second
        first = jnp.where(same, -1, first)
        second = jnp.where(same, -1, second)
        total = jnp.zeros((2 * rows, ew), jnp.float32)
        base = lax.broadcasted_iota(jnp.int16, (kb, ew), 0)
        for k in range(wide // kb):
            plus = base == (first - k * kb).astype(jnp.int16)
            minus = base == (second - k * kb).astype(jnp.int16)
            tile = jnp.where(plus, one, jnp.where(minus, -one, zero))
            inc[k * kb : (k + 1) * kb, cols] = tile
            if k * kb < nodes:
                total = total + dot(volt[:, k * kb : (k + 1) * kb], tile)
        partial[:, cols] = total[:rows] + total[rows:]
        return carry

    lax.fori_loop(0, elems // ew, build, 0)

    seen[dom] = v_ref[:, :border]
    for j in range(1, doms):
        v_copy(j, xor(dom, j, doms)).wait_recv()
    for p in range(doms):
        high, low = split(seen[p])
        volt[:rows, nodes + p * border : nodes + (p + 1) * border] = high
        volt[rows:, nodes + p * border : nodes + (p + 1) * border] = low

    def evaluate(i, carry):
        cols = pl.ds(pl.multiple_of(i * ew, ew), ew)
        total = dot(volt[:, nodes:], inc[nodes:, cols])
        across = partial[:, cols] + (total[:rows] + total[rows:])
        current = cur_ref[0:1, cols] * across + cur_ref[1:2, cols] * jnp.tanh(2.0 * across)
        charge = chg_ref[0:1, cols] * across + chg_ref[1:2, cols] * jnp.tanh(across)
        high, low = split(current)
        flow[:rows, cols] = high
        flow[rows : 2 * rows, cols] = low
        high, low = split(charge)
        flow[2 * rows : 3 * rows, cols] = high
        flow[3 * rows :, cols] = low
        return carry

    lax.fori_loop(0, elems // ew, evaluate, 0)

    def scatter(start, width):
        total = dot(flow[...], inc[pl.ds(pl.multiple_of(start, LANES), width), :], ((1,), (1,)))
        cur = total[:rows] + total[rows : 2 * rows]
        chg = total[2 * rows : 3 * rows] + total[3 * rows :]
        return [
            jnp.concatenate([cur[:, c * LANES : (c + 1) * LANES], chg[:, c * LANES : (c + 1) * LANES]], axis=1)
            for c in range(width // LANES)
        ]

    per = kb // LANES

    def border_block(i, carry):
        pieces = scatter(nodes + i * kb, kb)
        for c in range(per):
            edge_out[i * per + c] = pieces[c]
        return carry

    def peer_of(j):
        return xor(mine, j, near)

    def piece(index):
        return pl.ds(pl.multiple_of(index * rows, rows), rows)

    def out_copy(c, j, sender):
        peer = peer_of(j)
        return pltpu.make_async_remote_copy(
            src_ref=stage.at[c, peer],
            dst_ref=land.at[c, piece(sender), :],
            send_sem=out_send.at[c, j],
            recv_sem=out_recv.at[c, sender],
            device_id={"freq": half * near + peer},
            device_id_type=MESH,
        )

    order = []
    for b in range(group // kb - 1, -1, -1):
        order += [b * per + c for c in range(per)]

        def node_block(i, carry):
            peer = near - 1 - i
            j = xor(mine, peer, near)
            if b == group // kb - 1:
                @pl.when(i == 1)
                def _():
                    lax.fori_loop(0, (wide - nodes) // kb, border_block, 0)
                    for k in range(doms - 1, 0, -1):
                        edge_copy(k, xor(dom, k, doms), dom).start()

            pieces = scatter(peer * group + b * kb, kb)
            for c in range(per):
                stage[b * per + c, peer] = pieces[c]
            if b == 0:
                @pl.when(peer == 0)
                def _():
                    for k in range(1, doms):
                        edge_copy(k, dom, xor(dom, k, doms)).wait_recv()
                    total = stage[0, 0] + edge_out[dom]
                    for p in range(doms):
                        total = total + jnp.where(dom == p, 0.0, edge[p])
                    stage[0, 0] = total

            @pl.when(j != 0)
            def _():
                for c in range(per):
                    out_copy(b * per + c, j, mine).start()

            return carry

        lax.fori_loop(0, near, node_block, 0)

    def back_columns(c, sender):
        return pl.ds(pl.multiple_of((sender * chunks + c) * LANES, LANES), LANES)

    def back_copy(c, j, target, sender):
        return pltpu.make_async_remote_copy(
            src_ref=joined.at[c, piece(target), :],
            dst_ref=back.at[:, back_columns(c, sender)],
            send_sem=back_send.at[c, j],
            recv_sem=back_recv.at[c, sender],
            device_id={"freq": half * near + peer_of(j)},
            device_id_type=MESH,
        )

    span = near * rows

    def half_rows(which):
        return pl.ds(pl.multiple_of(which * span, span), span)

    def mirror_copy(c):
        return pltpu.make_async_remote_copy(
            src_ref=spec.at[c, half_rows(1 - half), :],
            dst_ref=mirror.at[c],
            send_sem=mirror_send.at[c],
            recv_sem=mirror_recv.at[c],
            device_id={"freq": mirror_id},
            device_id_type=MESH,
        )

    for load in loads:
        load.wait()
    row = lax.broadcasted_iota(jnp.int32, (samples, LANES), 0)
    rate = (row // 2).astype(jnp.float32) * (2.0 / samples)
    rate = jnp.where(row % 2 == 0, rate, -rate)

    def transform(c):
        land[c, piece(mine), :] = stage[c, mine]

        def arrived(i, carry):
            out_copy(c, near - 1 - i, peer_of(near - 1 - i)).wait_recv()
            return carry

        lax.fori_loop(0, near - 1, arrived, 0)
        high, low = split(land[c])
        big = high_ref[:, half_rows(half)]
        product = dot(big, high) + (dot(big, low) + dot(low_ref[:, half_rows(half)], high))
        spec[c] = product[:, :LANES] + rate * swap_pairs(product[:, LANES:])
        mirror_copy(c).start()

    def join(c):
        mirror_copy(c).wait_recv()
        joined[c] = spec[c, half_rows(half), :] + mirror[c]

        def give(i, carry):
            j = near - 1 - i
            back_copy(c, j, peer_of(j), mine).start()
            return carry

        lax.fori_loop(0, near - 1, give, 0)
        back[:, back_columns(c, mine)] = joined[c, piece(mine), :]

    for i, c in enumerate(order):
        transform(c)
        if i:
            join(order[i - 1])
    join(order[-1])

    even = lax.broadcasted_iota(jnp.int32, (rows, LANES), 0) % 2 == 0
    sums = (jnp.zeros((8, LANES), jnp.float32), jnp.zeros((8, LANES), jnp.float32))

    def fold(x):
        return jnp.sum((x * x).reshape(rows // 8, 8, LANES), axis=0)

    for c in order:
        def finish(j, carry):
            peer = peer_of(j)

            @pl.when(j != 0)
            def _():
                back_copy(c, j, peer, peer).wait_recv()

            cols = back_columns(c, peer)
            residual = back[:, cols] - src_ref[:, cols]
            upper = jnp.where(even, residual, pltpu.roll(residual, 1, 0))
            lower = jnp.where(even, pltpu.roll(residual, rows - 1, 0), residual)
            raw = -(jac_ref[:, 0, cols] * upper + jac_ref[:, 1, cols] * lower)
            back[:, cols] = residual
            raw_ref[:, cols] = raw
            return carry[0] + fold(raw), carry[1] + fold(residual)

        sums = lax.fori_loop(0, near, finish, sums)

    stores = [
        pltpu.make_async_copy(a, out_any.at[i], store_sem.at[i]) for i, a in enumerate((back, raw_ref))
    ]
    for store in stores:
        store.start()

    def whole(x):
        return jnp.sum(jnp.sum(x, axis=0, keepdims=True), axis=1, keepdims=True)

    lane = lax.broadcasted_iota(jnp.int32, (8, LANES), 1)
    part_dom[dom] = jnp.where(lane == 0, whole(sums[0]), jnp.where(lane == 1, whole(sums[1]), 0.0))

    def part_copy(axis, count, me, part, send, recv, j, sender):
        return pltpu.make_async_remote_copy(
            src_ref=part.at[me],
            dst_ref=part.at[sender],
            send_sem=send.at[j],
            recv_sem=recv.at[sender],
            device_id={axis: xor(me, j, count)},
            device_id_type=MESH,
        )

    def reduce_over(axis, count, me, part, send, recv):
        for j in range(count - 1, 0, -1):
            part_copy(axis, count, me, part, send, recv, j, me).start()
        for j in range(count - 1, 0, -1):
            part_copy(axis, count, me, part, send, recv, j, xor(me, j, count)).wait_recv()
        return sum((part[i] for i in range(1, count)), part[0])

    part_freq[freq] = reduce_over("dom", doms, dom, part_dom, pd_send, pd_recv)
    both = reduce_over("freq", freqs, freq, part_freq, pf_send, pf_recv)
    raw_sum = jnp.sum(jnp.where(lane == 0, both, 0.0)[:1], axis=1, keepdims=True)
    res_sum = jnp.sum(jnp.where(lane == 1, both, 0.0)[:1], axis=1, keepdims=True)
    spread = jnp.sqrt(raw_sum / entries + 1e-06)
    scale_ref[...] = jnp.minimum(1.0, trust_radius / spread)
    norm_ref[...] = jnp.sqrt(res_sum)
    for store in stores:
        store.wait()

    for j in range(1, doms):
        v_copy(j, dom).wait_send()
        edge_copy(j, dom, dom).wait_send()
        part_copy("dom", doms, dom, part_dom, pd_send, pd_recv, j, dom).wait_send()

    for c in range(chunks):
        mirror_copy(c).wait_send()

    def drain(i, carry):
        j = i + 1
        for c in range(chunks):
            out_copy(c, j, mine).wait_send()
            back_copy(c, j, mine, mine).wait_send()
        return carry

    lax.fori_loop(0, near - 1, drain, 0)

    def drain_parts(i, carry):
        part_copy("freq", freqs, freq, part_freq, pf_send, pf_recv, i + 1, freq).wait_send()
        return carry

    lax.fori_loop(0, freqs - 1, drain_parts, 0)


def damp_kernel(both_ref, scale_ref, residual_ref, step_ref):
    residual_ref[...] = both_ref[0]
    step_ref[...] = both_ref[1] * scale_ref[...]


def body(doms, freqs, voltages, sources, terminals, elem_current, elem_charge, jacobi):
    rows, nodes = voltages.shape
    elems = terminals.shape[1]
    border = nodes // 16
    wide = nodes + doms * border
    samples = rows * freqs
    near = freqs // 2
    chunks = nodes // near // LANES
    f32, bf16 = jnp.float32, jnp.bfloat16
    dma = pltpu.SemaphoreType.DMA
    vmem = pl.BlockSpec(memory_space=VMEM)
    anywhere = pl.BlockSpec(memory_space=pl.ANY)
    high, low = fourier_matrix(samples)
    both, norm, scale = pl.pallas_call(
        functools.partial(kernel, doms, freqs, float(samples * nodes * doms)),
        out_shape=(
            jax.ShapeDtypeStruct((2, rows, nodes), f32),
            jax.ShapeDtypeStruct((1, 1), f32),
            jax.ShapeDtypeStruct((1, 1), f32),
        ),
        in_specs=[vmem] * 4 + [anywhere] * 4,
        out_specs=(anywhere, vmem, vmem),
        scratch_shapes=[
            VMEM((rows, nodes), f32),
            VMEM((rows, nodes), f32),
            VMEM((2 * rows, wide), bf16),
            VMEM((doms, rows, border), f32),
            VMEM((wide, elems), bf16),
            VMEM((rows, elems), f32),
            VMEM((4 * rows, elems), bf16),
            VMEM((chunks, near, rows, 2 * LANES), f32),
            VMEM((doms, rows, 2 * LANES), f32),
            VMEM((doms, rows, 2 * LANES), f32),
            VMEM((chunks, near * rows, 2 * LANES), f32),
            VMEM((chunks, samples, LANES), f32),
            VMEM((chunks, near * rows, LANES), f32),
            VMEM((chunks, near * rows, LANES), f32),
            VMEM((samples, samples), bf16),
            VMEM((samples, samples), bf16),
            VMEM((rows, nodes), f32),
            VMEM((rows, 2, nodes), f32),
            VMEM((doms, 8, LANES), f32),
            VMEM((freqs, 8, LANES), f32),
            dma((doms,)), dma((doms,)),
            dma((doms,)), dma((doms,)),
            dma((chunks, near)), dma((chunks, near)),
            dma((chunks,)), dma((chunks,)),
            dma((chunks, near)), dma((chunks, near)),
            dma((doms,)), dma((doms,)),
            dma((freqs,)), dma((freqs,)),
            dma((4,)),
            dma((2,)),
        ],
        compiler_params=pltpu.CompilerParams(
            collective_id=0, has_side_effects=True, vmem_limit_bytes=60 * 1024 * 1024
        ),
    )(
        voltages, terminals, elem_current, elem_charge,
        jnp.asarray(high), jnp.asarray(low), sources, jacobi.reshape(rows, 2, nodes),
    )
    part = pl.BlockSpec((rows // 2, nodes), lambda i: (i, 0))
    residual, step = pl.pallas_call(
        damp_kernel,
        grid=(2,),
        out_shape=(jax.ShapeDtypeStruct((rows, nodes), f32),) * 2,
        in_specs=[
            pl.BlockSpec((2, rows // 2, nodes), lambda i: (0, i, 0)),
            pl.BlockSpec((1, 1), lambda i: (0, 0)),
        ],
        out_specs=(part, part),
    )(both, scale)
    return residual, step, norm.reshape(())


def solution(mesh):
    placed = (
        P("freq", "dom"),
        P("freq", "dom"),
        P(None, "dom"),
        P(None, "dom"),
        P(None, "dom"),
        P("freq", None, None, "dom"),
    )
    return jax.shard_map(
        functools.partial(body, mesh.shape["dom"], mesh.shape["freq"]),
        mesh=mesh,
        in_specs=placed,
        out_specs=(P("freq", "dom"), P("freq", "dom"), P()),
        check_vma=False,
    )
```

```python
import functools
import math

import jax
import jax.numpy as jnp
import numpy as np
from jax import lax
from jax.experimental import pallas as pl
from jax.experimental.pallas import tpu as pltpu
from jax.sharding import PartitionSpec as P

MESH = pl.DeviceIdType.MESH
LANES = 128
VMEM = pltpu.VMEM
trust_radius = 2.0


def fourier_matrix(samples):
    row = np.arange(samples)
    harmonic = row // 2
    sine = row % 2 == 1
    order = np.where(harmonic == 0, np.where(sine, samples // 2, 0), harmonic)
    phase = (order[:, None] * np.arange(samples)[None, :] % samples) * (2.0 * math.pi / samples)
    values = np.where((sine & (harmonic > 0))[:, None], np.sin(phase), np.cos(phase))
    weight = np.where(harmonic == 0, math.sqrt(1.0 / samples), math.sqrt(2.0 / samples))
    full = (values * weight[:, None]).astype(np.float32)
    high = full.astype(jnp.bfloat16)
    low = (full - high.astype(np.float32)).astype(jnp.bfloat16)
    return high, low


def split(x):
    high = x.astype(jnp.bfloat16)
    low = (x - high.astype(jnp.float32)).astype(jnp.bfloat16)
    return high, low


def dot(a, b, contract=((1,), (0,))):
    return lax.dot_general(a, b, (contract, ((), ())), preferred_element_type=jnp.float32)


def xor(a, b, count):
    out, bit = 0, 1
    while bit < count:
        out = out + bit * ((a // bit + b // bit) % 2)
        bit *= 2
    return out


def swap_pairs(x):
    even = lax.broadcasted_iota(jnp.int32, x.shape, 0) % 2 == 0
    rows = x.shape[0]
    return jnp.where(even, pltpu.roll(x, rows - 1, 0), pltpu.roll(x, 1, 0))


def kernel(
    doms, freqs, entries,
    v_ref, term_ref, cur_ref, chg_ref, high_any, low_any, src_any, jac_any,
    out_any, norm_ref, scale_ref,
    back, raw_ref, volt, seen, inc, partial, flow, stage, edge_out, edge, land, spec, mirror, joined, high_ref, low_ref, src_ref,
    jac_ref, part_dom, part_freq,
    v_send, v_recv, edge_send, edge_recv, out_send, out_recv, mirror_send, mirror_recv, back_send, back_recv,
    pd_send, pd_recv, pf_send, pf_recv, load_sem, store_sem,
):
    dom = lax.axis_index("dom")
    freq = lax.axis_index("freq")
    rows, nodes = v_ref.shape
    wide, elems = inc.shape
    border = seen.shape[2]
    samples = rows * freqs
    near = freqs // 2
    half = freq // near
    mine = freq % near
    mirror_id = freq + near * (1 - 2 * half)
    group = nodes // near
    chunks = group // LANES
    ew = 512
    kb = 256
    one, zero = jnp.bfloat16(1.0), jnp.bfloat16(0.0)

    barrier = pltpu.get_barrier_semaphore()
    for j in range(1, doms):
        pl.semaphore_signal(barrier, inc=1, device_id={"dom": xor(dom, j, doms)}, device_id_type=MESH)
    for j in range(1, freqs):
        pl.semaphore_signal(barrier, inc=1, device_id={"freq": xor(freq, j, freqs)}, device_id_type=MESH)

    loads = [
        pltpu.make_async_copy(a, b, load_sem.at[i])
        for i, (a, b) in enumerate(
            ((high_any, high_ref), (low_any, low_ref), (src_any, src_ref), (jac_any, jac_ref))
        )
    ]
    for load in loads:
        load.start()

    def dom_copy(j, source, target, send, recv, sender):
        return pltpu.make_async_remote_copy(
            src_ref=source,
            dst_ref=target.at[sender],
            send_sem=send.at[j],
            recv_sem=recv.at[sender],
            device_id={"dom": xor(dom, j, doms)},
            device_id_type=MESH,
        )

    def v_copy(j, sender):
        return dom_copy(j, v_ref.at[:, :border], seen, v_send, v_recv, sender)

    def edge_copy(j, owner, sender):
        return dom_copy(j, edge_out.at[owner], edge, edge_send, edge_recv, sender)

    high, low = split(v_ref[...])
    volt[:rows, :nodes] = high
    volt[rows:, :nodes] = low

    def build(i, carry):
        @pl.when(i == 1)
        def _():
            pl.semaphore_wait(barrier, doms + freqs - 2)
            for j in range(doms - 1, 0, -1):
                v_copy(j, dom).start()

        cols = pl.ds(pl.multiple_of(i * ew, ew), ew)
        first = term_ref[0:1, cols]
        second = term_ref[1:2, cols]
        same = first == second
        first = jnp.where(same, -1, first)
        second = jnp.where(same, -1, second)
        total = jnp.zeros((2 * rows, ew), jnp.float32)
        base = lax.broadcasted_iota(jnp.int16, (kb, ew), 0)
        for k in range(wide // kb):
            plus = base == (first - k * kb).astype(jnp.int16)
            minus = base == (second - k * kb).astype(jnp.int16)
            tile = jnp.where(plus, one, jnp.where(minus, -one, zero))
            inc[k * kb : (k + 1) * kb, cols] = tile
            if k * kb < nodes:
                total = total + dot(volt[:, k * kb : (k + 1) * kb], tile)
        partial[:, cols] = total[:rows] + total[rows:]
        return carry

    lax.fori_loop(0, elems // ew, build, 0)

    seen[dom] = v_ref[:, :border]
    for j in range(1, doms):
        v_copy(j, xor(dom, j, doms)).wait_recv()
    for p in range(doms):
        high, low = split(seen[p])
        volt[:rows, nodes + p * border : nodes + (p + 1) * border] = high
        volt[rows:, nodes + p * border : nodes + (p + 1) * border] = low

    def evaluate(i, carry):
        cols = pl.ds(pl.multiple_of(i * ew, ew), ew)
        total = dot(volt[:, nodes:], inc[nodes:, cols])
        across = partial[:, cols] + (total[:rows] + total[rows:])
        current = cur_ref[0:1, cols] * across + cur_ref[1:2, cols] * jnp.tanh(2.0 * across)
        charge = chg_ref[0:1, cols] * across + chg_ref[1:2, cols] * jnp.tanh(across)
        high, low = split(current)
        flow[:rows, cols] = high
        flow[rows : 2 * rows, cols] = low
        high, low = split(charge)
        flow[2 * rows : 3 * rows, cols] = high
        flow[3 * rows :, cols] = low
        return carry

    lax.fori_loop(0, elems // ew, evaluate, 0)

    def scatter(start, width):
        total = dot(flow[...], inc[pl.ds(pl.multiple_of(start, LANES), width), :], ((1,), (1,)))
        cur = total[:rows] + total[rows : 2 * rows]
        chg = total[2 * rows : 3 * rows] + total[3 * rows :]
        return [
            jnp.concatenate([cur[:, c * LANES : (c + 1) * LANES], chg[:, c * LANES : (c + 1) * LANES]], axis=1)
            for c in range(width // LANES)
        ]

    per = kb // LANES

    def border_block(i, carry):
        pieces = scatter(nodes + i * kb, kb)
        for c in range(per):
            edge_out[i * per + c] = pieces[c]
        return carry

    def peer_of(j):
        return xor(mine, j, near)

    def piece(index):
        return pl.ds(pl.multiple_of(index * rows, rows), rows)

    def out_copy(c, j, sender):
        peer = peer_of(j)
        return pltpu.make_async_remote_copy(
            src_ref=stage.at[c, peer],
            dst_ref=land.at[c, piece(sender), :],
            send_sem=out_send.at[c, j],
            recv_sem=out_recv.at[c, sender],
            device_id={"freq": half * near + peer},
            device_id_type=MESH,
        )

    def back_columns(c, sender):
        return pl.ds(pl.multiple_of((sender * chunks + c) * LANES, LANES), LANES)

    def back_copy(c, j, target, sender):
        return pltpu.make_async_remote_copy(
            src_ref=joined.at[c, piece(target), :],
            dst_ref=back.at[:, back_columns(c, sender)],
            send_sem=back_send.at[c, j],
            recv_sem=back_recv.at[c, sender],
            device_id={"freq": half * near + peer_of(j)},
            device_id_type=MESH,
        )

    span = near * rows

    def half_rows(which):
        return pl.ds(pl.multiple_of(which * span, span), span)

    def mirror_copy(c):
        return pltpu.make_async_remote_copy(
            src_ref=spec.at[c, half_rows(1 - half), :],
            dst_ref=mirror.at[c],
            send_sem=mirror_send.at[c],
            recv_sem=mirror_recv.at[c],
            device_id={"freq": mirror_id},
            device_id_type=MESH,
        )

    for load in loads:
        load.wait()
    row = lax.broadcasted_iota(jnp.int32, (samples, LANES), 0)
    rate = (row // 2).astype(jnp.float32) * (2.0 / samples)
    rate = jnp.where(row % 2 == 0, rate, -rate)

    def transform(c):
        land[c, piece(mine), :] = stage[c, mine]

        def arrived(i, carry):
            out_copy(c, near - 1 - i, peer_of(near - 1 - i)).wait_recv()
            return carry

        lax.fori_loop(0, near - 1, arrived, 0)
        high, low = split(land[c])
        big = high_ref[:, half_rows(half)]
        product = dot(big, high) + (dot(big, low) + dot(low_ref[:, half_rows(half)], high))
        spec[c] = product[:, :LANES] + rate * swap_pairs(product[:, LANES:])
        mirror_copy(c).start()

    def join(c):
        mirror_copy(c).wait_recv()
        joined[c] = spec[c, half_rows(half), :] + mirror[c]

        def give(i, carry):
            j = near - 1 - i
            back_copy(c, j, peer_of(j), mine).start()
            return carry

        lax.fori_loop(0, near - 1, give, 0)
        back[:, back_columns(c, mine)] = joined[c, piece(mine), :]

    order = []
    for b in range(group // kb - 1, -1, -1):
        order += [b * per + c for c in range(per)]

        def node_block(i, carry):
            peer = near - 1 - i
            j = xor(mine, peer, near)
            if b == group // kb - 1:
                @pl.when(i == 1)
                def _():
                    lax.fori_loop(0, (wide - nodes) // kb, border_block, 0)
                    for k in range(doms - 1, 0, -1):
                        edge_copy(k, xor(dom, k, doms), dom).start()

            pieces = scatter(peer * group + b * kb, kb)
            for c in range(per):
                stage[b * per + c, peer] = pieces[c]
            if b == 0:
                @pl.when(peer == 0)
                def _():
                    for k in range(1, doms):
                        edge_copy(k, dom, xor(dom, k, doms)).wait_recv()
                    total = stage[0, 0] + edge_out[dom]
                    for p in range(doms):
                        total = total + jnp.where(dom == p, 0.0, edge[p])
                    stage[0, 0] = total

            @pl.when(j != 0)
            def _():
                for c in range(per):
                    out_copy(b * per + c, j, mine).start()

            return carry

        early = order[:-per] if b == 0 else []
        lax.fori_loop(0, near // 2, node_block, 0)
        for c in early:
            transform(c)
        lax.fori_loop(near // 2, near, node_block, 0)

    waiting = order[:-per]
    for c in order[-per:]:
        if waiting:
            join(waiting.pop(0))
        transform(c)
        waiting.append(c)
    for c in waiting:
        join(c)

    even = lax.broadcasted_iota(jnp.int32, (rows, LANES), 0) % 2 == 0
    sums = (jnp.zeros((8, LANES), jnp.float32), jnp.zeros((8, LANES), jnp.float32))

    def fold(x):
        return jnp.sum((x * x).reshape(rows // 8, 8, LANES), axis=0)

    for c in order:
        def finish(j, carry):
            peer = peer_of(j)

            @pl.when(j != 0)
            def _():
                back_copy(c, j, peer, peer).wait_recv()

            cols = back_columns(c, peer)
            residual = back[:, cols] - src_ref[:, cols]
            upper = jnp.where(even, residual, pltpu.roll(residual, 1, 0))
            lower = jnp.where(even, pltpu.roll(residual, rows - 1, 0), residual)
            raw = -(jac_ref[:, 0, cols] * upper + jac_ref[:, 1, cols] * lower)
            back[:, cols] = residual
            raw_ref[:, cols] = raw
            return carry[0] + fold(raw), carry[1] + fold(residual)

        sums = lax.fori_loop(0, near, finish, sums)

    stores = [
        pltpu.make_async_copy(a, out_any.at[i], store_sem.at[i]) for i, a in enumerate((back, raw_ref))
    ]
    for store in stores:
        store.start()

    def whole(x):
        return jnp.sum(jnp.sum(x, axis=0, keepdims=True), axis=1, keepdims=True)

    lane = lax.broadcasted_iota(jnp.int32, (8, LANES), 1)
    part_dom[dom] = jnp.where(lane == 0, whole(sums[0]), jnp.where(lane == 1, whole(sums[1]), 0.0))

    def part_copy(axis, count, me, part, send, recv, j, sender):
        return pltpu.make_async_remote_copy(
            src_ref=part.at[me],
            dst_ref=part.at[sender],
            send_sem=send.at[j],
            recv_sem=recv.at[sender],
            device_id={axis: xor(me, j, count)},
            device_id_type=MESH,
        )

    def reduce_over(axis, count, me, part, send, recv):
        for j in range(count - 1, 0, -1):
            part_copy(axis, count, me, part, send, recv, j, me).start()
        for j in range(count - 1, 0, -1):
            part_copy(axis, count, me, part, send, recv, j, xor(me, j, count)).wait_recv()
        return sum((part[i] for i in range(1, count)), part[0])

    part_freq[freq] = reduce_over("dom", doms, dom, part_dom, pd_send, pd_recv)
    both = reduce_over("freq", freqs, freq, part_freq, pf_send, pf_recv)
    raw_sum = jnp.sum(jnp.where(lane == 0, both, 0.0)[:1], axis=1, keepdims=True)
    res_sum = jnp.sum(jnp.where(lane == 1, both, 0.0)[:1], axis=1, keepdims=True)
    spread = jnp.sqrt(raw_sum / entries + 1e-06)
    scale_ref[...] = jnp.minimum(1.0, trust_radius / spread)
    norm_ref[...] = jnp.sqrt(res_sum)
    for store in stores:
        store.wait()

    for j in range(1, doms):
        v_copy(j, dom).wait_send()
        edge_copy(j, dom, dom).wait_send()
        part_copy("dom", doms, dom, part_dom, pd_send, pd_recv, j, dom).wait_send()

    for c in range(chunks):
        mirror_copy(c).wait_send()

    def drain(i, carry):
        j = i + 1
        for c in range(chunks):
            out_copy(c, j, mine).wait_send()
            back_copy(c, j, mine, mine).wait_send()
        return carry

    lax.fori_loop(0, near - 1, drain, 0)

    def drain_parts(i, carry):
        part_copy("freq", freqs, freq, part_freq, pf_send, pf_recv, i + 1, freq).wait_send()
        return carry

    lax.fori_loop(0, freqs - 1, drain_parts, 0)


def damp_kernel(both_ref, scale_ref, residual_ref, step_ref):
    residual_ref[...] = both_ref[0]
    step_ref[...] = both_ref[1] * scale_ref[...]


def body(doms, freqs, voltages, sources, terminals, elem_current, elem_charge, jacobi):
    rows, nodes = voltages.shape
    elems = terminals.shape[1]
    border = nodes // 16
    wide = nodes + doms * border
    samples = rows * freqs
    near = freqs // 2
    chunks = nodes // near // LANES
    f32, bf16 = jnp.float32, jnp.bfloat16
    dma = pltpu.SemaphoreType.DMA
    vmem = pl.BlockSpec(memory_space=VMEM)
    anywhere = pl.BlockSpec(memory_space=pl.ANY)
    high, low = fourier_matrix(samples)
    both, norm, scale = pl.pallas_call(
        functools.partial(kernel, doms, freqs, float(samples * nodes * doms)),
        out_shape=(
            jax.ShapeDtypeStruct((2, rows, nodes), f32),
            jax.ShapeDtypeStruct((1, 1), f32),
            jax.ShapeDtypeStruct((1, 1), f32),
        ),
        in_specs=[vmem] * 4 + [anywhere] * 4,
        out_specs=(anywhere, vmem, vmem),
        scratch_shapes=[
            VMEM((rows, nodes), f32),
            VMEM((rows, nodes), f32),
            VMEM((2 * rows, wide), bf16),
            VMEM((doms, rows, border), f32),
            VMEM((wide, elems), bf16),
            VMEM((rows, elems), f32),
            VMEM((4 * rows, elems), bf16),
            VMEM((chunks, near, rows, 2 * LANES), f32),
            VMEM((doms, rows, 2 * LANES), f32),
            VMEM((doms, rows, 2 * LANES), f32),
            VMEM((chunks, near * rows, 2 * LANES), f32),
            VMEM((chunks, samples, LANES), f32),
            VMEM((chunks, near * rows, LANES), f32),
            VMEM((chunks, near * rows, LANES), f32),
            VMEM((samples, samples), bf16),
            VMEM((samples, samples), bf16),
            VMEM((rows, nodes), f32),
            VMEM((rows, 2, nodes), f32),
            VMEM((doms, 8, LANES), f32),
            VMEM((freqs, 8, LANES), f32),
            dma((doms,)), dma((doms,)),
            dma((doms,)), dma((doms,)),
            dma((chunks, near)), dma((chunks, near)),
            dma((chunks,)), dma((chunks,)),
            dma((chunks, near)), dma((chunks, near)),
            dma((doms,)), dma((doms,)),
            dma((freqs,)), dma((freqs,)),
            dma((4,)),
            dma((2,)),
        ],
        compiler_params=pltpu.CompilerParams(
            collective_id=0, has_side_effects=True, vmem_limit_bytes=60 * 1024 * 1024
        ),
    )(
        voltages, terminals, elem_current, elem_charge,
        jnp.asarray(high), jnp.asarray(low), sources, jacobi.reshape(rows, 2, nodes),
    )
    part = pl.BlockSpec((rows // 2, nodes), lambda i: (i, 0))
    residual, step = pl.pallas_call(
        damp_kernel,
        grid=(2,),
        out_shape=(jax.ShapeDtypeStruct((rows, nodes), f32),) * 2,
        in_specs=[
            pl.BlockSpec((2, rows // 2, nodes), lambda i: (0, i, 0)),
            pl.BlockSpec((1, 1), lambda i: (0, 0)),
        ],
        out_specs=(part, part),
    )(both, scale)
    return residual, step, norm.reshape(())


def solution(mesh):
    placed = (
        P("freq", "dom"),
        P("freq", "dom"),
        P(None, "dom"),
        P(None, "dom"),
        P(None, "dom"),
        P("freq", None, None, "dom"),
    )
    return jax.shard_map(
        functools.partial(body, mesh.shape["dom"], mesh.shape["freq"]),
        mesh=mesh,
        in_specs=placed,
        out_specs=(P("freq", "dom"), P("freq", "dom"), P()),
        check_vma=False,
    )
```
